32 devices in a mesh: cfg: 4 (over y, core), dom: 8 (over z, x).
Axes of the slice: x: 2, y: 2, z: 4, core: 2. Of those that a mesh axis runs over, the one named last changes fastest.
Arguments:
- features: bfloat16 [4, 12288, 512], P('cfg', 'dom'), may hold values from -6 to 6
- cotangent: bfloat16 [4, 12288, 512], P('cfg', 'dom'), may hold values from -6 to 6
- w_self: bfloat16 [512, 512], P('cfg'), may hold values from -0.25 to 0.25
- w_neigh: bfloat16 [512, 512], P('cfg'), may hold values from -0.25 to 0.25
- tiles: bfloat16 [64, 128, 128], P('dom'), may hold values from -0.3125 to 0.3125
- edge_peer: int32 [256, 1], P('dom'), may hold values from 0 to 7; in each aligned block of 32 rows (0 to 31, 32 to 63, ...) at most 8 rows name the same one
- edge_src: int32 [256], P('dom'), may hold values from 0 to 11
- edge_dst: int32 [256], P('dom'), may hold values from 0 to 11
- edge_tile: int32 [256], P('dom'), may hold values from 0 to 7
Outputs:
- hidden: bfloat16 [4, 12288, 512], P('cfg', 'dom')
- grad_self: float32 [512, 512], P('cfg')
- grad_neigh: float32 [512, 512], P('cfg')
The draws below stay inside these ranges and needn't reach their ends.
Inputs may be any that keep to these rules, and one draw needn't show every extreme that they name: `edge_peer`: among the 32 edge blocks of one partition at most 8 have their destination on any one partition, and some destination partition takes exactly 8 of them.
All inputs are finite; a program needn't handle non-finite values.
Results may differ from the reference program's by a relative error of at most 0.0061.
Values may be sent and summed in bfloat16 or wider, within the bound.
No kernel may reach another device: no remote copies, remote signals or barrier semaphores. Data moves between devices by JAX's collectives and lax.ppermute only.
A program may use at most 128 MiB of HBM per device.

```python
import math
import jax
import jax.numpy as jnp
import numpy as np
from jax import lax

D = 512
TILE = 128
BLK_DEV = 12
EB_DEV = 32
TILES_DEV = 8
CAP = 8
CONFIGS = 4
NODES = 12288
N_DOM = 8


def plant(drawn, key, smallest, high):
    shape = drawn.shape
    index_at = [jax.random.randint(jax.random.fold_in(key, axis), (), 0, shape[axis]) for axis in range(len(shape))]
    drawn = drawn.at[tuple(index_at)].set(smallest)
    longest = shape.index(max(shape))
    index_at[longest] = (index_at[longest] + 1) % shape[longest]
    return drawn.at[tuple(index_at)].set(high)


def level_of(rng, shape, cuts, smallest, largest):
    def one(position, parts):
        steps = jax.random.uniform(jax.random.fold_in(jax.random.fold_in(rng, 6), position), (parts,), jnp.float32, smallest / len(cuts), largest / len(cuts))
        return jnp.repeat(jnp.exp(steps), shape[position] // parts).reshape((-1,) + (1,) * (len(shape) - position - 1))

    loudness = one(*cuts[0])
    for cut in cuts[1:]:
        loudness = loudness * one(*cut)
    return loudness


def routed_block(key, own, number, rows, count, top, bound, slope):
    sequence = jax.random.permutation(key, count)
    heavy_load, usual = portions_of(count, rows * top, bound, slope, True), portions_of(count, rows * top, bound, slope, False)
    places = jnp.arange(count)

    def named(sizes, offset_by):
        used = int((sizes > 0).sum())
        fixed = max(1, used // 4)
        shifted = fixed + (places - fixed + offset_by * (used - fixed)) % max(1, count - fixed)
        return jnp.zeros((count,), jnp.int32).at[sequence[jnp.where(places < fixed, places, shifted)]].set(jnp.asarray(sizes, jnp.int32))

    sizes = jnp.where(number % 4 == 0, named(heavy_load, number // 4), named(usual, number - number // 4 - 1))
    mixed = jax.random.permutation(jax.random.fold_in(own, 3), count)
    donor, taker = mixed[0:count // 2 * 2:2], mixed[1:count // 2 * 2:2]
    slack = jnp.minimum(sizes[donor] - 1, bound - sizes[taker]) // 2
    slack = jnp.where((donor == sequence[0]) | (taker == sequence[0]) | (sizes[taker] == 0), 0, jnp.maximum(slack, 0))
    shifted = jax.random.randint(jax.random.fold_in(own, 4), (count // 2,), 0, 1 << 20) % (slack + 1)
    sizes = sizes.at[donor].add(-shifted).at[taker].add(shifted)
    labels = jnp.searchsorted(jnp.cumsum(sizes), jnp.arange(rows * top), side="right").astype(jnp.int32)
    listing = labels.reshape(top, rows).T
    listing = listing[jax.random.permutation(jax.random.fold_in(own, 1), rows)]
    offset_by = jax.random.randint(jax.random.fold_in(own, 2), (rows, 1), 0, top)
    return jnp.take_along_axis(listing, (jnp.arange(top)[None, :] + offset_by) % top, axis=1)


def portions_of(amount, total, limit, skew, full):
    weights = [(1 << 20) // math.isqrt(standing ** skew) + 1 for standing in range(1, amount + 1)]
    largest = limit if full else min(limit, max(-(-total // amount), total * weights[0] // sum(weights)))
    least = 1 if total - largest >= amount - 1 else 0
    holding, rest = [largest] + [least] * (amount - 1), total - largest - least * (amount - 1)
    while rest > 0:
        free = [i for i in range(1, amount) if holding[i] < largest] or [i for i in range(1, amount) if holding[i] < limit]
        mass, budget = sum([weights[i] for i in free]), rest
        for i in free:
            more = min(limit - holding[i], max(1, budget * weights[i] // mass), rest)
            holding[i] = holding[i] + more
            rest = rest - more
    return np.array(holding)


def centred(stream_key, extent, deviation, most, split=(), kind=jnp.bfloat16):
    result = jax.random.normal(stream_key, extent, jnp.float32) * deviation
    if len(split) > 0:
        result = level_of(stream_key, extent, split, -0.22, 0.18) * result
    return jnp.clip(result, min=-most, max=most).astype(kind)


def setup_inputs(seed: int = 0) -> dict:
    splits = jax.random.split(jax.random.key(seed), 10)
    features = centred(splits[0], (CONFIGS, NODES, D), 1.0, 6.0, ((0, 4), (1, 8)))
    cotangent = centred(splits[1], (CONFIGS, NODES, D), 1.0, 6.0, ((0, 4), (1, 8)))
    w_self = centred(splits[2], (D, D), D ** -0.5, 0.25, ((0, 4),))
    w_neigh = centred(splits[3], (D, D), D ** -0.5, 0.25, ((0, 4),))
    tiles = centred(splits[4], (N_DOM * TILES_DEV, TILE, TILE), (TILE * EB_DEV // BLK_DEV) ** -0.5, 0.3125, ((0, 8),))
    edge_peer_keys = jax.random.split(jax.random.fold_in(splits[5], 1), (N_DOM * EB_DEV) // EB_DEV)
    edge_peer_turns = jax.random.permutation(jax.random.fold_in(splits[5], 3), (N_DOM * EB_DEV) // EB_DEV)
    edge_peer = jax.vmap(lambda own, number: routed_block(jax.random.fold_in(splits[5], 2), own, number, EB_DEV, N_DOM, 1, CAP, 2))(edge_peer_keys, edge_peer_turns).reshape((N_DOM * EB_DEV, 1))
    edge_src = plant(jax.random.randint(splits[6], (N_DOM * EB_DEV,), 0, BLK_DEV), jax.random.fold_in(splits[6], 1), 0, BLK_DEV - 1).astype(jnp.int32)
    edge_dst = plant(jax.random.randint(splits[7], (N_DOM * EB_DEV,), 0, BLK_DEV), jax.random.fold_in(splits[7], 1), 0, BLK_DEV - 1).astype(jnp.int32)
    edge_tile = plant(jax.random.randint(splits[8], (N_DOM * EB_DEV,), 0, TILES_DEV), jax.random.fold_in(splits[8], 1), 0, TILES_DEV - 1).astype(jnp.int32)
    return dict(features=features, cotangent=cotangent, w_self=w_self, w_neigh=w_neigh, tiles=tiles, edge_peer=edge_peer, edge_src=edge_src, edge_dst=edge_dst, edge_tile=edge_tile)


def head(pre):
    normed = pre * lax.rsqrt(lax.optimization_barrier(jnp.mean(pre * pre, -1, keepdims=True)) + 1e-05)
    return normed * jax.nn.sigmoid(normed)

def reference(features, cotangent, w_self, w_neigh, tiles, edge_peer, edge_src, edge_dst, edge_tile):
    edges = N_DOM * EB_DEV
    nblocks = N_DOM * BLK_DEV
    owner = (jnp.arange(edges, dtype=jnp.int32) // EB_DEV).astype(jnp.int32)
    src_block = (owner * BLK_DEV + edge_src).astype(jnp.int32)
    dst_block = (edge_peer[:, 0] * BLK_DEV + edge_dst).astype(jnp.int32)
    chosen_tiles = tiles[(owner * TILES_DEV + edge_tile).astype(jnp.int32)].astype(jnp.float32)

    def one(carry, pair):
        feats, cot = pair
        blocks_x = feats.reshape(nblocks, TILE, D)
        chosen = blocks_x[src_block].astype(jnp.float32)
        partial_value = jnp.einsum('etk,ekd->etd', chosen_tiles, chosen).astype(jnp.bfloat16)
        summed = jax.ops.segment_sum(partial_value.astype(jnp.float32), dst_block, num_segments=nblocks)
        aggregate = summed.reshape(nblocks * TILE, D).astype(jnp.bfloat16)
        pre = jnp.dot(feats, w_self, preferred_element_type=jnp.float32) + jnp.dot(aggregate, w_neigh, preferred_element_type=jnp.float32)
        out, pullback = jax.vjp(head, pre)
        grad_pre = pullback(cot.astype(jnp.float32))[0].astype(jnp.bfloat16)
        term_s = lax.dot_general(feats, grad_pre, (((0,), (0,)), ((), ())), preferred_element_type=jnp.float32)
        term_n = lax.dot_general(aggregate, grad_pre, (((0,), (0,)), ((), ())), preferred_element_type=jnp.float32)
        return ((carry[0] + term_s, carry[1] + term_n), out.astype(jnp.bfloat16))
    start = (jnp.zeros((D, D), jnp.float32), jnp.zeros((D, D), jnp.float32))
    totals, hidden = lax.scan(one, start, (features, cotangent))
    factor = float(CONFIGS * NODES) ** (-0.5)
    return (hidden, totals[0] * factor, totals[1] * factor)
```

```python
import functools

import jax
import jax.numpy as jnp
from jax import lax
from jax.experimental import pallas as pl
from jax.experimental.pallas import tpu as pltpu
from jax.sharding import PartitionSpec as P


def head(pre):
    normed = pre * lax.rsqrt(jnp.mean(pre * pre, -1, keepdims=True) + 1e-05)
    return normed * jax.nn.sigmoid(normed)


def swap(value, axis, bit):
    size = lax.axis_size(axis)
    return lax.ppermute(value, axis, [(i, i ^ bit) for i in range(size)])


def bits(axis):
    size = lax.axis_size(axis)
    assert size & (size - 1) == 0
    return [1 << k for k in range(size.bit_length() - 1)]


def gather_xor(value, axis, order):
    held, offsets = value, [0]
    for bit in order:
        held = jnp.concatenate([held, swap(held, axis, bit)], 0)
        offsets = offsets + [offset ^ bit for offset in offsets]
    return held, offsets


def in_order(held, offsets, axis):
    own = lax.axis_index(axis)
    slot_of = jnp.zeros((len(offsets),), jnp.int32)
    place = [offsets.index(j) for j in range(len(offsets))]
    picks = jnp.asarray(place, jnp.int32)[jnp.arange(len(offsets)) ^ own]
    return held[picks]


def edges_kernel(group, meta, x_ref, tiles_ref, out_ref, acc_ref):
    owners, width, rows = x_ref.shape
    tile = tiles_ref.shape[1]
    blocks = rows // tile
    edges = meta.shape[1]
    acc_ref[...] = jnp.zeros_like(acc_ref)

    def body(step, carry):
        values = []
        for i in range(group):
            e = step * group + i
            source = x_ref[meta[0, e], :, pl.ds(pl.multiple_of(meta[1, e] * tile, tile), tile)]
            values.append(
                lax.dot_general(
                    source,
                    tiles_ref[meta[3, e]],
                    (((1,), (1,)), ((), ())),
                    preferred_element_type=jnp.float32,
                )
            )
        for i in range(group):
            e = step * group + i
            acc_ref[meta[2, e]] += values[i]
        return carry

    lax.fori_loop(0, edges // group, body, 0)
    for owner in range(owners):
        for block in range(blocks):
            out_ref[owner, :, block * tile : (block + 1) * tile] = acc_ref[
                owner * blocks + block
            ].astype(out_ref.dtype)


def sum_edges(meta, x, tiles):
    owners, width, rows = x.shape
    tile = tiles.shape[1]
    edges = meta.shape[1]
    group = 8 if edges % 8 == 0 else 1
    return pl.pallas_call(
        functools.partial(edges_kernel, group),
        out_shape=jax.ShapeDtypeStruct(x.shape, x.dtype),
        grid_spec=pltpu.PrefetchScalarGridSpec(
            num_scalar_prefetch=1,
            grid=(),
            in_specs=[pl.BlockSpec(memory_space=pltpu.VMEM)] * 2,
            out_specs=pl.BlockSpec(memory_space=pltpu.VMEM),
            scratch_shapes=[pltpu.VMEM((owners * rows // tile, width, tile), jnp.float32)],
        ),
        cost_estimate=pl.CostEstimate(
            flops=2 * edges * tile * tile * width,
            bytes_accessed=2 * x.size * 2 + tiles.size * 2,
            transcendentals=0,
        ),
    )(meta, x, tiles)


def local(features, cotangent, w_self, w_neigh, tiles, edge_peer, edge_src, edge_dst, edge_tile):
    feats = features[0]
    rows, width = feats.shape
    count, tile, _ = tiles.shape
    blocks = rows // tile
    edges = edge_src.shape[0]
    peers = lax.axis_size("dom")
    configs = lax.axis_size("cfg")
    mine = lax.axis_index("cfg")
    bf16, f32 = jnp.bfloat16, jnp.float32
    part = width // peers

    moved = lax.all_to_all(
        feats.T.reshape(peers, part, rows), "dom", split_axis=0, concat_axis=0, tiled=True
    )

    lanes = -(-4 * edges // tile)
    info = jnp.concatenate([edge_peer[:, 0], edge_src, edge_dst, edge_tile]).astype(bf16)
    info = jnp.pad(info, (0, lanes * tile - 4 * edges)).reshape(lanes, tile)
    piece = count * tile // configs
    own_rows = lax.dynamic_slice_in_dim(tiles.reshape(count * tile, tile), mine * piece, piece, 0)
    spare = -(-lanes // 16) * 16
    packed = jnp.concatenate([own_rows, jnp.pad(info, ((0, spare - lanes), (0, 0)))], 0)
    held, offsets = gather_xor(packed[None], "dom", bits("dom")[::-1])
    held = in_order(held, offsets, "dom")
    infos = (
        held[:, piece : piece + lanes].reshape(peers, lanes * tile)[:, : 4 * edges].reshape(peers, 4, edges)
    )
    infos = infos.astype(jnp.int32)
    owner = jnp.broadcast_to(jnp.arange(peers, dtype=jnp.int32)[:, None], (peers, edges))
    meta = jnp.stack(
        [
            owner.reshape(-1),
            infos[:, 1].reshape(-1),
            (infos[:, 0] * blocks + infos[:, 2]).reshape(-1),
            (owner * count + infos[:, 3]).reshape(-1),
        ]
    )
    pieces, offsets = gather_xor(held[:, :piece][None], "cfg", bits("cfg")[::-1])
    pieces = in_order(pieces, offsets, "cfg")
    all_tiles = pieces.swapaxes(0, 1).reshape(peers * count, tile, tile)

    weights, offsets = gather_xor(jnp.concatenate([w_self, w_neigh], 1)[None], "cfg", bits("cfg")[::-1])
    weights = in_order(weights, offsets, "cfg").reshape(width, 2 * width)

    summed = sum_edges(meta, moved, all_tiles)
    back = lax.all_to_all(summed, "dom", split_axis=0, concat_axis=0, tiled=True)
    aggregate = back.reshape(width, rows)

    pre = jnp.dot(feats, weights[:, :width], preferred_element_type=f32) + lax.dot_general(
        aggregate, weights[:, width:], (((0,), (0,)), ((), ())), preferred_element_type=f32
    )
    out, pullback = jax.vjp(head, pre)
    grad_pre = pullback(cotangent[0].astype(f32))[0].astype(bf16)
    factor = float(configs * peers * rows) ** (-0.5)
    term_s = lax.dot_general(feats, grad_pre, (((0,), (0,)), ((), ())), preferred_element_type=f32)
    term_n = jnp.dot(aggregate, grad_pre, preferred_element_type=f32)

    def reduce(term, order):
        held = term.reshape(configs, width // configs, width)
        for bit in bits("cfg"):
            pairs = held.reshape((held.shape[0] // 2, 2) + held.shape[1:])
            side = (mine // bit) % 2
            keep = lax.dynamic_index_in_dim(pairs, side, 1, keepdims=False)
            give = lax.dynamic_index_in_dim(pairs, 1 - side, 1, keepdims=False)
            held = keep + swap(give.astype(bf16), "cfg", bit).astype(f32)
        held = held[0]
        for bit in order:
            held = held + swap(held.astype(bf16), "dom", bit).astype(f32)
        return held * factor

    steps = bits("dom")
    grad_s = reduce(term_s, steps)
    grad_n = reduce(term_n, steps[1:] + steps[:1])
    return (out.astype(bf16)[None], grad_s, grad_n)


def solution(mesh):
    placed = (
        P("cfg", "dom", None),
        P("cfg", "dom", None),
        P("cfg", None),
        P("cfg", None),
        P("dom", None, None),
        P("dom", None),
        P("dom"),
        P("dom"),
        P("dom"),
    )
    return jax.shard_map(
        local,
        mesh=mesh,
        in_specs=placed,
        out_specs=(P("cfg", "dom", None), P("cfg", None), P("cfg", None)),
        check_vma=False,
    )
```

```python
import functools

import jax
import jax.numpy as jnp
from jax import lax
from jax.experimental import pallas as pl
from jax.experimental.pallas import tpu as pltpu
from jax.sharding import PartitionSpec as P


BF16, F32, I32 = jnp.bfloat16, jnp.float32, jnp.int32
WHOLE = pl.BlockSpec(memory_space=pltpu.VMEM)
LANES = 128


def swap(value, axis, bits):
    size = lax.axis_size(axis)
    return lax.ppermute(value, axis, [(i, i ^ bits) for i in range(size)])


def bits_of(axis):
    size = lax.axis_size(axis)
    assert size & (size - 1) == 0
    return [1 << k for k in range(size.bit_length() - 1)]


def pack_kernel(at, tiles_ref, peer_ref, src_ref, dst_ref, tile_ref, packed_ref, turned_ref, info_ref):
    count, tile, _ = tiles_ref.shape
    piece = packed_ref.shape[0] - info_ref.shape[0]
    edges = src_ref.shape[1]
    if piece % tile == 0:
        for i in range(piece // tile):
            packed_ref[i * tile : (i + 1) * tile] = tiles_ref[at[1] * (piece // tile) + i].T
    else:
        for i in range(count):
            turned_ref[i * tile : (i + 1) * tile] = tiles_ref[i].T
        packed_ref[:piece] = turned_ref[pl.ds(pl.multiple_of(at[1] * piece, piece), piece)]
    info_ref[...] = jnp.zeros_like(info_ref)
    for row, ref in enumerate((peer_ref, src_ref, dst_ref, tile_ref)):
        info_ref[row : row + 1, :edges] = ref[...].astype(F32)
    packed_ref[piece:] = info_ref[...].astype(BF16)


def turn_kernel(at, feats_ref, *refs):
    *out_refs, turned_ref = refs
    rows, half = feats_ref.shape
    slots = len(out_refs)
    part = half // slots
    step = 256 if rows % 256 == 0 else rows
    for i in range(rows // step):
        turned_ref[:, i * step : (i + 1) * step] = feats_ref[i * step : (i + 1) * step].T
    for k, out_ref in enumerate(out_refs):
        start = pl.multiple_of(((at[0] % slots) ^ k) * part, part)
        out_ref[...] = turned_ref[pl.ds(start, part)]


def turn_half(at, feats, peers, far):
    rows, width = feats.shape
    slots = peers // 2
    return pl.pallas_call(
        turn_kernel,
        out_shape=[jax.ShapeDtypeStruct((width // peers, rows), BF16)] * slots,
        grid_spec=pltpu.PrefetchScalarGridSpec(
            num_scalar_prefetch=1,
            grid=(1,),
            in_specs=[pl.BlockSpec((rows, width // 2), lambda i, at: (0, (at[0] // slots) ^ far))],
            out_specs=[WHOLE] * slots,
            scratch_shapes=[pltpu.VMEM((width // 2, rows), BF16)],
        ),
        compiler_params=pltpu.CompilerParams(vmem_limit_bytes=12 << 20),
        cost_estimate=pl.CostEstimate(flops=0, bytes_accessed=2 * rows * width, transcendentals=0),
    )(at, feats)


def reverse_bits(value, size):
    out = jnp.zeros_like(value)
    bit = 1
    while bit < size:
        out = out * 2 + (value // bit) % 2
        bit *= 2
    return out


def edges_kernel(slots, first, chunks, at, meta, *refs):
    x_refs = refs[: len(slots)]
    tiles_ref = refs[len(slots)]
    rest = refs[len(slots) + 1 :]
    tile = LANES
    edges = meta.shape[2]
    _, rows = x_refs[0].shape
    blocks = rows // tile
    if first and chunks:
        out_refs, acc_ref = rest[:-1], rest[-1]
        acc_ref[...] = jnp.zeros_like(acc_ref)
    elif first:
        acc_ref = rest[0]
        acc_ref[...] = jnp.zeros_like(acc_ref)
    else:
        out_refs, acc_ref = rest[1:-1], rest[-1]
        acc_ref[...] = rest[0][...]
    for slot, x_ref in zip(slots, x_refs):
        for base in range(0, edges, 32):
            values = []
            for e in range(base, min(base + 32, edges)):
                source = x_ref[:, pl.ds(pl.multiple_of(meta[slot, 0, e], tile), tile)]
                value = jnp.dot(source, tiles_ref[meta[slot, 2, e]], preferred_element_type=F32)
                values.append(value.astype(BF16).astype(F32))
            for i, value in enumerate(values):
                acc_ref[meta[slot, 1, base + i]] += value
    span = blocks // max(chunks, 1)
    peers = meta.shape[0]
    for chunk in range(chunks):
        for k in range(peers):
            start = (at[0] ^ k) * blocks + chunk * span
            for block in range(span):
                out_refs[chunk * peers + k][:, block * tile : (block + 1) * tile] = acc_ref[
                    start + block
                ].astype(BF16)


def sum_edges(at, meta, xs, slots, tiles, held, chunks):
    part, rows = xs[0].shape
    peers, _, edges = meta.shape
    total = (peers * (rows // LANES), part, LANES)
    if chunks:
        shapes = [jax.ShapeDtypeStruct((part, rows // chunks), BF16)] * (chunks * peers)
        scratch = [pltpu.VMEM(total, F32)]
    else:
        shapes, scratch = [jax.ShapeDtypeStruct(total, F32)], []
    operands = list(xs) + [tiles] + ([] if held is None else [held])
    return pl.pallas_call(
        functools.partial(edges_kernel, slots, held is None, chunks),
        out_shape=shapes,
        grid_spec=pltpu.PrefetchScalarGridSpec(
            num_scalar_prefetch=2,
            grid=(),
            in_specs=[WHOLE] * len(operands),
            out_specs=[WHOLE] * len(shapes),
            scratch_shapes=scratch,
        ),
        compiler_params=pltpu.CompilerParams(vmem_limit_bytes=24 << 20),
        cost_estimate=pl.CostEstimate(
            flops=2 * len(slots) * edges * LANES * LANES * part,
            bytes_accessed=2 * len(slots) * (part * rows + 8 * LANES * LANES),
            transcendentals=0,
        ),
    )(at, meta, *operands)


def head_kernel(peers, first, last, at, *refs):
    a_refs = refs[:peers]
    feats_ref, cot_ref, weights_ref = refs[peers : peers + 3]
    refs = refs[peers + 3 :]
    if not first:
        held_s, held_n = refs[1:3]
        refs = refs[3:]
    if last:
        out_ref, keep_s, keep_n, give_s, give_n, agg_ref, sum_s, sum_n = refs
    else:
        out_ref, sum_s, sum_n, agg_ref = refs
    width = feats_ref.shape[1]
    step = feats_ref.shape[0]
    i = pl.program_id(0)

    @pl.when(i == 0)
    def _():
        part = width // peers
        for k in range(peers):
            agg_ref[pl.ds(pl.multiple_of((at[0] ^ k) * part, part), part)] = a_refs[k][...]
        sum_s[...] = jnp.zeros_like(sum_s) if first else held_s[...]
        sum_n[...] = jnp.zeros_like(sum_n) if first else held_n[...]

    feats = feats_ref[...]
    agg = agg_ref[:, pl.ds(pl.multiple_of(i * step, step), step)]
    over_rows = (((0,), (0,)), ((), ()))
    pre = jnp.dot(feats, weights_ref[:, :width], preferred_element_type=F32)
    pre += lax.dot_general(agg, weights_ref[:, width:], over_rows, preferred_element_type=F32)
    scale = lax.rsqrt(jnp.mean(pre * pre, -1, keepdims=True) + 1e-05)
    normed = pre * scale
    gate = jax.nn.sigmoid(normed)
    out_ref[...] = (normed * gate).astype(BF16)
    slope = cot_ref[...].astype(F32) * (gate * (1.0 + normed * (1.0 - gate)))
    grad = scale * (slope - normed * jnp.mean(slope * normed, -1, keepdims=True))
    grad = grad.astype(BF16)
    sum_s[...] += lax.dot_general(feats, grad, over_rows, preferred_element_type=F32)
    sum_n[...] += jnp.dot(agg, grad, preferred_element_type=F32)

    if last:

        @pl.when(i == pl.num_programs(0) - 1)
        def _():
            pairs, share, _ = keep_s.shape
            side = at[1] % 2
            for total, keep, give in ((sum_s, keep_s, give_s), (sum_n, keep_n, give_n)):
                for pair in range(pairs):
                    here = pl.multiple_of((2 * pair + side) * share, share)
                    there = pl.multiple_of((2 * pair + 1 - side) * share, share)
                    keep[pair] = total[pl.ds(here, share)]
                    give[pair] = total[pl.ds(there, share)].astype(BF16)


def run_head(at, parts, feats, cot, weights, hidden, held, chunk, chunks, configs):
    rows, width = feats.shape
    span = rows // chunks
    step = 256 if span % 256 == 0 else 128
    steps = span // step
    base = chunk * steps
    by_rows = pl.BlockSpec((step, width), lambda i, at: (base + i, 0))
    first, last = chunk == 0, chunk == chunks - 1
    shapes = [jax.ShapeDtypeStruct((rows, width), BF16)]
    out_specs = [by_rows]
    sums = (width, width)
    scratch = [pltpu.VMEM((width, span), BF16)]
    peers = len(parts)
    if last:
        share = (configs // 2, width // configs, width)
        shapes += [jax.ShapeDtypeStruct(share, F32)] * 2 + [jax.ShapeDtypeStruct(share, BF16)] * 2
        out_specs += [WHOLE] * 4
        scratch += [pltpu.VMEM(sums, F32)] * 2
    else:
        shapes += [jax.ShapeDtypeStruct(sums, F32)] * 2
        out_specs += [WHOLE] * 2
    return pl.pallas_call(
        functools.partial(head_kernel, peers, first, last),
        out_shape=shapes,
        grid_spec=pltpu.PrefetchScalarGridSpec(
            num_scalar_prefetch=1,
            grid=(steps,),
            in_specs=[WHOLE] * peers
            + [by_rows, by_rows, WHOLE]
            + ([] if first else [pl.BlockSpec(memory_space=pl.ANY), WHOLE, WHOLE]),
            out_specs=out_specs,
            scratch_shapes=scratch,
        ),
        input_output_aliases={} if first else {peers + 4: 0},
        compiler_params=pltpu.CompilerParams(vmem_limit_bytes=24 << 20),
        cost_estimate=pl.CostEstimate(
            flops=8 * span * width * width, bytes_accessed=8 * span * width, transcendentals=span * width
        ),
    )(at, *parts, feats, cot, weights, *(() if first else (hidden, *held)))


def local(features, cotangent, w_self, w_neigh, tiles, edge_peer, edge_src, edge_dst, edge_tile):
    return layer(
        features[0], cotangent[0], w_self, w_neigh, tiles, edge_peer, edge_src, edge_dst, edge_tile
    )


def layer(feats, cot, w_self, w_neigh, tiles, edge_peer, edge_src, edge_dst, edge_tile):
    rows, width = feats.shape
    count, tile, _ = tiles.shape
    edges = edge_src.shape[0]
    assert tile == LANES and edges <= LANES
    peers = lax.axis_size("dom")
    configs = lax.axis_size("cfg")
    assert configs % 2 == 0 and peers % 2 == 0
    own = lax.axis_index("cfg")
    at = jnp.stack([lax.axis_index("dom"), own]).astype(I32)
    blocks = rows // tile
    chunks = 2 if blocks % 2 == 0 else 1
    dom_bits, cfg_bits = bits_of("dom"), bits_of("cfg")
    middle = peers // 2

    piece = count * tile // configs
    packed = pl.pallas_call(
        pack_kernel,
        out_shape=jax.ShapeDtypeStruct((piece + 16, tile), BF16),
        grid_spec=pltpu.PrefetchScalarGridSpec(
            num_scalar_prefetch=1,
            grid=(),
            in_specs=[WHOLE] * 5,
            out_specs=WHOLE,
            scratch_shapes=[pltpu.VMEM((count * tile, tile), BF16), pltpu.VMEM((16, tile), F32)],
        ),
        compiler_params=pltpu.CompilerParams(vmem_limit_bytes=8 << 20),
        name="pack",
    )(
        at,
        tiles,
        edge_peer.reshape(1, edges),
        edge_src.reshape(1, edges),
        edge_dst.reshape(1, edges),
        edge_tile.reshape(1, edges),
    )
    far_turned = turn_half(at, feats, peers, 1)
    near_turned = turn_half(at, feats, peers, 0)

    held, offsets = packed[None], [0]
    for bit in dom_bits[::-1]:
        held = jnp.concatenate([held, swap(held, "dom", bit)], 0)
        offsets = offsets + [k ^ bit for k in offsets]
    slot = {k: offsets.index(k) for k in range(peers)}
    quarters = held[:, :piece]
    pieces = jnp.concatenate([quarters[None], swap(quarters[None], "cfg", cfg_bits[-1])], 0)
    for bit in cfg_bits[:-1][::-1]:
        pieces = jnp.concatenate([pieces, swap(pieces, "cfg", bit)], 0)

    infos = held[:, piece : piece + 4, :edges].astype(I32)
    slot_of = jnp.arange(peers, dtype=I32)[:, None]
    if piece % tile == 0:
        per = piece // tile
        owner = reverse_bits((infos[:, 3] // per) ^ own, configs)
        which = (owner * peers + slot_of) * per + infos[:, 3] % per
        all_tiles = pieces.reshape(peers * count, tile, tile)
    else:
        which = slot_of * count + infos[:, 3]
        order = reverse_bits(jnp.arange(configs, dtype=I32) ^ own, configs)
        all_tiles = pieces[order].swapaxes(0, 1).reshape(peers * count, tile, tile)
    meta = jnp.stack([infos[:, 1] * tile, infos[:, 0] * blocks + infos[:, 2], which], 1)

    moved = {0: near_turned[0]}
    for k in range(1, peers):
        block = far_turned[k - middle] if k >= middle else near_turned[k]
        moved[k] = swap(block, "dom", k)

    weights = jnp.concatenate([w_self, w_neigh], 1)[None]
    for bit in cfg_bits[::-1]:
        weights = jnp.concatenate([weights, swap(weights, "cfg", bit)], 0)
    order = reverse_bits(jnp.arange(configs, dtype=I32) ^ own, configs)
    weights = weights[order].reshape(width, 2 * width)

    near, far = list(range(middle)), list(range(middle, peers))
    partly = sum_edges(at, meta, [moved[k] for k in near], [slot[k] for k in near], all_tiles, None, 0)[0]
    summed = sum_edges(at, meta, [moved[k] for k in far], [slot[k] for k in far], all_tiles, partly, chunks)
    held = hidden = None
    for chunk in range(chunks):
        parts = summed[chunk * peers : (chunk + 1) * peers]
        back = [parts[0]] + [swap(parts[k], "dom", k) for k in range(1, peers)]
        hidden, *held = run_head(
            at, back, feats, cot, weights, hidden, held, chunk, chunks, configs
        )
    keep_s, keep_n, give_s, give_n = held
    factor = float(configs * peers * rows) ** (-0.5)

    def reduce(keep, give, order):
        total = keep + swap(give, "cfg", cfg_bits[0]).astype(F32)
        for bit in cfg_bits[1:]:
            pairs = total.reshape((total.shape[0] // 2, 2) + total.shape[1:])
            side = (own // bit) % 2
            keep = lax.dynamic_index_in_dim(pairs, side, 1, keepdims=False)
            give = lax.dynamic_index_in_dim(pairs, 1 - side, 1, keepdims=False)
            total = keep + swap(give.astype(BF16), "cfg", bit).astype(F32)
        total = total[0]
        for bit in order:
            total = total + swap(total.astype(BF16), "dom", bit).astype(F32)
        return total * factor

    grad_s = reduce(keep_s, give_s, dom_bits)
    grad_n = reduce(keep_n, give_n, dom_bits[1:] + dom_bits[:1])
    return (hidden[None], grad_s, grad_n)


def solution(mesh):
    placed = (
        P("cfg", "dom", None),
        P("cfg", "dom", None),
        P("cfg", None),
        P("cfg", None),
        P("dom", None, None),
        P("dom", None),
        P("dom"),
        P("dom"),
        P("dom"),
    )
    return jax.shard_map(
        local,
        mesh=mesh,
        in_specs=placed,
        out_specs=(P("cfg", "dom", None), P("cfg", None), P("cfg", None)),
        check_vma=False,
    )
```

```python
import functools

import jax
import jax.numpy as jnp
from jax import lax
from jax.experimental import pallas as pl
from jax.experimental.pallas import tpu as pltpu
from jax.sharding import PartitionSpec as P


BF16, F32, I32 = jnp.bfloat16, jnp.float32, jnp.int32
WHOLE = pl.BlockSpec(memory_space=pltpu.VMEM)
STAYS = pl.BlockSpec(memory_space=pltpu.HBM)
LANES = 128


def swap(value, axis, bits):
    size = lax.axis_size(axis)
    return lax.ppermute(value, axis, [(i, i ^ bits) for i in range(size)])


def bits_of(axis):
    size = lax.axis_size(axis)
    assert size & (size - 1) == 0
    return [1 << k for k in range(size.bit_length() - 1)]


def pack_kernel(at, tiles_hbm, peer, src, dst, name, packed_ref, tiles_ref, turned_ref, lists_ref, info_ref, sem):
    per, tile, _ = tiles_ref.shape
    piece = packed_ref.shape[0] - info_ref.shape[0]
    edges = src.shape[1]
    first = at[1] * per if per < tiles_hbm.shape[0] else 0
    fetches = [pltpu.make_async_copy(tiles_hbm.at[pl.ds(first, per)], tiles_ref, sem.at[0])]
    for row, ref in enumerate((peer, src, dst, name)):
        fetches.append(pltpu.make_async_copy(ref, lists_ref.at[row], sem.at[1 + row]))
    for fetch in fetches:
        fetch.start()
    info_ref[...] = jnp.zeros_like(info_ref)
    for fetch in fetches:
        fetch.wait()
    if per < tiles_hbm.shape[0]:
        for i in range(per):
            packed_ref[i * tile : (i + 1) * tile] = tiles_ref[i].T
    else:
        for i in range(per):
            turned_ref[i * tile : (i + 1) * tile] = tiles_ref[i].T
        packed_ref[:piece] = turned_ref[pl.ds(pl.multiple_of(at[1] * piece, piece), piece)]
    for row in range(4):
        info_ref[row : row + 1, :edges] = lists_ref[row].astype(F32)
    packed_ref[piece:] = info_ref[...].astype(BF16)


def turn_kernel(at, feats_ref, *refs):
    *out_refs, turned_ref = refs
    rows, half = feats_ref.shape
    slots = len(out_refs)
    part = half // slots
    step = 256 if rows % 256 == 0 else rows
    for i in range(rows // step):
        turned_ref[:, i * step : (i + 1) * step] = feats_ref[i * step : (i + 1) * step].T
    for k, out_ref in enumerate(out_refs):
        start = pl.multiple_of(((at[0] % slots) ^ k) * part, part)
        out_ref[...] = turned_ref[pl.ds(start, part)]


def turn_half(at, feats, peers, far):
    rows, width = feats.shape
    slots = peers // 2
    return pl.pallas_call(
        turn_kernel,
        out_shape=[jax.ShapeDtypeStruct((width // peers, rows), BF16)] * slots,
        grid_spec=pltpu.PrefetchScalarGridSpec(
            num_scalar_prefetch=1,
            grid=(1,),
            in_specs=[pl.BlockSpec((rows, width // 2), lambda i, at: (0, (at[0] // slots) ^ far))],
            out_specs=[WHOLE] * slots,
            scratch_shapes=[pltpu.VMEM((width // 2, rows), BF16)],
        ),
        compiler_params=pltpu.CompilerParams(vmem_limit_bytes=12 << 20),
        cost_estimate=pl.CostEstimate(flops=0, bytes_accessed=2 * rows * width, transcendentals=0),
    )(at, feats)


def reverse_bits(value, size):
    out = jnp.zeros_like(value)
    bit = 1
    while bit < size:
        out = out * 2 + (value // bit) % 2
        bit *= 2
    return out


def edges_kernel(slots, first, chunks, at, meta, *refs):
    x_refs = refs[: len(slots)]
    tiles_ref = refs[len(slots)]
    rest = refs[len(slots) + 1 :]
    tile = LANES
    edges = meta.shape[2]
    _, rows = x_refs[0].shape
    blocks = rows // tile
    if first and chunks:
        out_refs, acc_ref = rest[:-1], rest[-1]
        acc_ref[...] = jnp.zeros_like(acc_ref)
    elif first:
        acc_ref = rest[0]
        acc_ref[...] = jnp.zeros_like(acc_ref)
    else:
        out_refs, acc_ref = rest[1:-1], rest[-1]
        acc_ref[...] = rest[0][...]
    for slot, x_ref in zip(slots, x_refs):
        for base in range(0, edges, 32):
            values = []
            for e in range(base, min(base + 32, edges)):
                source = x_ref[:, pl.ds(pl.multiple_of(meta[slot, 0, e], tile), tile)]
                value = jnp.dot(source, tiles_ref[meta[slot, 2, e]], preferred_element_type=F32)
                values.append(value.astype(BF16).astype(F32))
            for i, value in enumerate(values):
                acc_ref[meta[slot, 1, base + i]] += value
    span = blocks // max(chunks, 1)
    peers = meta.shape[0]
    for chunk in range(chunks):
        for k in range(peers):
            start = (at[0] ^ k) * blocks + chunk * span
            for block in range(span):
                out_refs[chunk * peers + k][:, block * tile : (block + 1) * tile] = acc_ref[
                    start + block
                ].astype(BF16)


def sum_edges(at, meta, xs, slots, tiles, held, chunks):
    part, rows = xs[0].shape
    peers, _, edges = meta.shape
    total = (peers * (rows // LANES), part, LANES)
    if chunks:
        shapes = [jax.ShapeDtypeStruct((part, rows // chunks), BF16)] * (chunks * peers)
        scratch = [pltpu.VMEM(total, F32)]
    else:
        shapes, scratch = [jax.ShapeDtypeStruct(total, F32)], []
    operands = list(xs) + [tiles] + ([] if held is None else [held])
    return pl.pallas_call(
        functools.partial(edges_kernel, slots, held is None, chunks),
        out_shape=shapes,
        grid_spec=pltpu.PrefetchScalarGridSpec(
            num_scalar_prefetch=2,
            grid=(),
            in_specs=[WHOLE] * len(operands),
            out_specs=[WHOLE] * len(shapes),
            scratch_shapes=scratch,
        ),
        compiler_params=pltpu.CompilerParams(vmem_limit_bytes=24 << 20),
        cost_estimate=pl.CostEstimate(
            flops=2 * len(slots) * edges * LANES * LANES * part,
            bytes_accessed=2 * len(slots) * (part * rows + 8 * LANES * LANES),
            transcendentals=0,
        ),
    )(at, meta, *operands)


def head_kernel(peers, base, first, last, at, *refs):
    a_refs = refs[:peers]
    feats_ref, cot_ref, weights_ref = refs[peers : peers + 3]
    refs = refs[peers + 3 :]
    if not first:
        held = refs[1:3]
        refs = refs[3:]
    count = 5 if last else 3
    out_ref, *sum_refs = refs[:count]
    agg_ref, x_ref, c_ref, w_ref, pre_ref, made_ref, grad_ref, *refs = refs[count:]
    totals, in_sem, out_sem = refs[:2], refs[2], refs[3]
    if last:
        gives = refs[4:6]
    width, span = agg_ref.shape
    part = width // peers
    step = 256 if span % 256 == 0 else 128
    stores = []

    def fetch(source, place, slot):
        copy = pltpu.make_async_copy(source, place, in_sem.at[slot])
        copy.start()
        return copy

    def store(source, place):
        copy = pltpu.make_async_copy(source, place, out_sem.at[len(stores)])
        copy.start()
        stores.append(copy)

    own_rows = pl.ds(base, span)
    early = [fetch(feats_ref.at[own_rows], x_ref, peers), fetch(weights_ref, w_ref, peers + 1)]
    parts = []
    for k in range(peers):
        place = agg_ref.at[pl.ds(pl.multiple_of((at[0] ^ k) * part, part), part)]
        parts.append(fetch(a_refs[k], place, k))
    parts.append(fetch(cot_ref.at[own_rows], c_ref, peers + 2))
    late = []
    if not first:
        late = [fetch(ref, total, peers + 3 + i) for i, (ref, total) in enumerate(zip(held, totals))]
    for copy in early:
        copy.wait()
    pre_ref[...] = jnp.dot(x_ref[...], w_ref[:, :width], preferred_element_type=F32)
    for copy in parts:
        copy.wait()

    over_rows = (((0,), (0,)), ((), ()))
    for i in range(span // step):
        here = slice(i * step, (i + 1) * step)
        pre = pre_ref[here] + lax.dot_general(
            agg_ref[:, here], w_ref[:, width:], over_rows, preferred_element_type=F32
        )
        scale = lax.rsqrt(jnp.mean(pre * pre, -1, keepdims=True) + 1e-05)
        normed = pre * scale
        gate = jax.nn.sigmoid(normed)
        made_ref[here] = (normed * gate).astype(BF16)
        store(made_ref.at[here], out_ref.at[base + i * step : base + (i + 1) * step])
        slope = c_ref[here].astype(F32)
        slope = slope * (gate * (1.0 + normed * (1.0 - gate)))
        grad = scale * (slope - normed * jnp.mean(slope * normed, -1, keepdims=True))
        grad_ref[here] = grad.astype(BF16)

    for copy in late:
        copy.wait()
    grad = grad_ref[...]
    for i, total in enumerate(totals):
        if i == 0:
            term = lax.dot_general(x_ref[...], grad, over_rows, preferred_element_type=F32)
        else:
            term = jnp.dot(agg_ref[...], grad, preferred_element_type=F32)
        total[...] = term if first else total[...] + term
        if not last:
            store(total, sum_refs[i])
            continue
        keep, give = sum_refs[i], sum_refs[2 + i]
        pairs, share, _ = keep.shape
        side = at[1] % 2
        for pair in range(pairs):
            here = pl.multiple_of((2 * pair + side) * share, share)
            there = pl.multiple_of((2 * pair + 1 - side) * share, share)
            gives[i][pair] = total[pl.ds(there, share)].astype(BF16)
            store(total.at[pl.ds(here, share)], keep.at[pair])
        store(gives[i], give)
    for copy in stores:
        copy.wait()


def run_head(at, parts, feats, cot, weights, hidden, held, base, span, configs):
    peers = len(parts)
    rows, width = feats.shape
    first, last = base == 0, base + span == rows
    step = 256 if span % 256 == 0 else 128
    shapes = [jax.ShapeDtypeStruct((rows, width), BF16)]
    sums = (width, width)
    scratch = [
        pltpu.VMEM((width, span), BF16),
        pltpu.VMEM((span, width), BF16),
        pltpu.VMEM((span, width), BF16),
        pltpu.VMEM((width, 2 * width), BF16),
        pltpu.VMEM((span, width), F32),
        pltpu.VMEM((span, width), BF16),
        pltpu.VMEM((span, width), BF16),
        pltpu.VMEM(sums, F32),
        pltpu.VMEM(sums, F32),
        pltpu.SemaphoreType.DMA((peers + 5,)),
        pltpu.SemaphoreType.DMA((span // step + (2 + configs if last else 2),)),
    ]
    if last:
        share = (configs // 2, width // configs, width)
        shapes += [jax.ShapeDtypeStruct(share, F32)] * 2 + [jax.ShapeDtypeStruct(share, BF16)] * 2
        scratch += [pltpu.VMEM(share, BF16)] * 2
    else:
        shapes += [jax.ShapeDtypeStruct(sums, F32)] * 2
    operands = [*parts, feats, cot, weights] + ([] if first else [hidden, *held])
    return pl.pallas_call(
        functools.partial(head_kernel, peers, base, first, last),
        out_shape=shapes,
        grid_spec=pltpu.PrefetchScalarGridSpec(
            num_scalar_prefetch=1,
            grid=(),
            in_specs=[STAYS] * len(operands),
            out_specs=[STAYS] * len(shapes),
            scratch_shapes=scratch,
        ),
        input_output_aliases={} if first else {peers + 4: 0},
        compiler_params=pltpu.CompilerParams(vmem_limit_bytes=60 << 20),
        cost_estimate=pl.CostEstimate(
            flops=8 * span * width * width, bytes_accessed=8 * span * width, transcendentals=span * width
        ),
    )(at, *operands)


def local(features, cotangent, w_self, w_neigh, tiles, edge_peer, edge_src, edge_dst, edge_tile):
    return layer(
        features[0], cotangent[0], w_self, w_neigh, tiles, edge_peer, edge_src, edge_dst, edge_tile
    )


def layer(feats, cot, w_self, w_neigh, tiles, edge_peer, edge_src, edge_dst, edge_tile):
    rows, width = feats.shape
    count, tile, _ = tiles.shape
    edges = edge_src.shape[0]
    assert tile == LANES and edges <= LANES
    peers = lax.axis_size("dom")
    configs = lax.axis_size("cfg")
    assert configs % 2 == 0 and peers % 2 == 0
    own = lax.axis_index("cfg")
    at = jnp.stack([lax.axis_index("dom"), own]).astype(I32)
    blocks = rows // tile
    chunks = 2 if blocks % 2 == 0 else 1
    dom_bits, cfg_bits = bits_of("dom"), bits_of("cfg")
    middle = peers // 2

    piece = count * tile // configs
    per = piece // tile if piece % tile == 0 else count
    pack = pl.pallas_call(
        pack_kernel,
        out_shape=jax.ShapeDtypeStruct((piece + 16, tile), BF16),
        grid_spec=pltpu.PrefetchScalarGridSpec(
            num_scalar_prefetch=1,
            grid=(),
            in_specs=[STAYS] * 5,
            out_specs=WHOLE,
            scratch_shapes=[
                pltpu.VMEM((per, tile, tile), BF16),
                pltpu.VMEM((count * tile, tile), BF16),
                pltpu.VMEM((4, 1, edges), I32),
                pltpu.VMEM((16, tile), F32),
                pltpu.SemaphoreType.DMA((5,)),
            ],
        ),
        compiler_params=pltpu.CompilerParams(vmem_limit_bytes=60 << 20),
        name="pack",
    )
    lists = [each.reshape(1, edges) for each in (edge_peer, edge_src, edge_dst, edge_tile)]
    packed = pack(at, tiles, *lists)
    far_turned = turn_half(at, feats, peers, 1)
    near_turned = turn_half(at, feats, peers, 0)

    held, offsets = packed[None], [0]
    for bit in dom_bits[::-1]:
        held = jnp.concatenate([held, swap(held, "dom", bit)], 0)
        offsets = offsets + [k ^ bit for k in offsets]
    slot = {k: offsets.index(k) for k in range(peers)}
    quarters = held[:, :piece]
    pieces = jnp.concatenate([quarters[None], swap(quarters[None], "cfg", cfg_bits[-1])], 0)
    for bit in cfg_bits[:-1][::-1]:
        pieces = jnp.concatenate([pieces, swap(pieces, "cfg", bit)], 0)

    infos = held[:, piece : piece + 4, :edges].astype(I32)
    slot_of = jnp.arange(peers, dtype=I32)[:, None]
    if piece % tile == 0:
        owner = reverse_bits((infos[:, 3] // per) ^ own, configs)
        which = (owner * peers + slot_of) * per + infos[:, 3] % per
        all_tiles = pieces.reshape(peers * count, tile, tile)
    else:
        which = slot_of * count + infos[:, 3]
        order = reverse_bits(jnp.arange(configs, dtype=I32) ^ own, configs)
        all_tiles = pieces[order].swapaxes(0, 1).reshape(peers * count, tile, tile)
    meta = jnp.stack([infos[:, 1] * tile, infos[:, 0] * blocks + infos[:, 2], which], 1)

    moved = {0: near_turned[0]}
    for k in range(1, peers):
        block = far_turned[k - middle] if k >= middle else near_turned[k]
        moved[k] = swap(block, "dom", k)

    weights = jnp.concatenate([w_self, w_neigh], 1)[None]
    for bit in cfg_bits[::-1]:
        weights = jnp.concatenate([weights, swap(weights, "cfg", bit)], 0)
    order = reverse_bits(jnp.arange(configs, dtype=I32) ^ own, configs)
    weights = weights[order].reshape(width, 2 * width)

    near, far = list(range(middle)), list(range(middle, peers))
    partly = sum_edges(at, meta, [moved[k] for k in near], [slot[k] for k in near], all_tiles, None, 0)[0]
    summed = sum_edges(at, meta, [moved[k] for k in far], [slot[k] for k in far], all_tiles, partly, chunks)
    held = hidden = None
    span = rows // chunks
    for chunk in range(chunks):
        parts = summed[chunk * peers : (chunk + 1) * peers]
        back = [parts[0]] + [swap(parts[k], "dom", k) for k in range(1, peers)]
        hidden, *held = run_head(
            at, back, feats, cot, weights, hidden, held, chunk * span, span, configs
        )
    keep_s, keep_n, give_s, give_n = held
    factor = float(configs * peers * rows) ** (-0.5)

    def reduce(keep, give, order):
        total = keep + swap(give, "cfg", cfg_bits[0]).astype(F32)
        for bit in cfg_bits[1:]:
            pairs = total.reshape((total.shape[0] // 2, 2) + total.shape[1:])
            side = (own // bit) % 2
            keep = lax.dynamic_index_in_dim(pairs, side, 1, keepdims=False)
            give = lax.dynamic_index_in_dim(pairs, 1 - side, 1, keepdims=False)
            total = keep + swap(give.astype(BF16), "cfg", bit).astype(F32)
        total = total[0]
        for bit in order:
            total = total + swap(total.astype(BF16), "dom", bit).astype(F32)
        return total * factor

    grad_s = reduce(keep_s, give_s, dom_bits)
    grad_n = reduce(keep_n, give_n, dom_bits[1:] + dom_bits[:1])
    return (hidden[None], grad_s, grad_n)


def solution(mesh):
    placed = (
        P("cfg", "dom", None),
        P("cfg", "dom", None),
        P("cfg", None),
        P("cfg", None),
        P("dom", None, None),
        P("dom", None),
        P("dom"),
        P("dom"),
        P("dom"),
    )
    return jax.shard_map(
        local,
        mesh=mesh,
        in_specs=placed,
        out_specs=(P("cfg", "dom", None), P("cfg", None), P("cfg", None)),
        check_vma=False,
    )
```

```python
import functools

import jax
import jax.numpy as jnp
from jax import lax
from jax.experimental import pallas as pl
from jax.experimental.pallas import tpu as pltpu
from jax.sharding import PartitionSpec as P


BF16, F32, I32 = jnp.bfloat16, jnp.float32, jnp.int32
WHOLE = pl.BlockSpec(memory_space=pltpu.VMEM)
STAYS = pl.BlockSpec(memory_space=pltpu.HBM)
LANES = 128


def swap(value, axis, bits):
    size = lax.axis_size(axis)
    return lax.ppermute(value, axis, [(i, i ^ bits) for i in range(size)])


def bits_of(axis):
    size = lax.axis_size(axis)
    assert size & (size - 1) == 0
    return [1 << k for k in range(size.bit_length() - 1)]


def pack_kernel(tiles_hbm, peer, src, dst, name, packed_ref, tiles_ref, turned_ref, lists_ref, info_ref, sem):
    per, tile, _ = tiles_ref.shape
    piece = packed_ref.shape[0] - info_ref.shape[0]
    edges = src.shape[1]
    own = lax.axis_index("cfg")
    first = own * per if per < tiles_hbm.shape[0] else 0
    fetches = [pltpu.make_async_copy(tiles_hbm.at[pl.ds(first, per)], tiles_ref, sem.at[0])]
    for row, ref in enumerate((peer, src, dst, name)):
        fetches.append(pltpu.make_async_copy(ref, lists_ref.at[row], sem.at[1 + row]))
    for fetch in fetches:
        fetch.start()
    info_ref[...] = jnp.zeros_like(info_ref)
    for fetch in fetches:
        fetch.wait()
    if per < tiles_hbm.shape[0]:
        for i in range(per):
            packed_ref[i * tile : (i + 1) * tile] = tiles_ref[i].T
    else:
        for i in range(per):
            turned_ref[i * tile : (i + 1) * tile] = tiles_ref[i].T
        packed_ref[:piece] = turned_ref[pl.ds(pl.multiple_of(own * piece, piece), piece)]
    for row in range(4):
        info_ref[row : row + 1, :edges] = lists_ref[row].astype(F32)
    packed_ref[piece:] = info_ref[...].astype(BF16)


def turn_kernel(at, feats_ref, *refs):
    *out_refs, turned_ref = refs
    rows, half = feats_ref.shape
    slots = len(out_refs)
    part = half // slots
    step = 256 if rows % 256 == 0 else rows
    for i in range(rows // step):
        turned_ref[:, i * step : (i + 1) * step] = feats_ref[i * step : (i + 1) * step].T
    for k, out_ref in enumerate(out_refs):
        start = pl.multiple_of(((at[0] % slots) ^ k) * part, part)
        out_ref[...] = turned_ref[pl.ds(start, part)]


def turn_half(at, feats, peers, far):
    rows, width = feats.shape
    slots = peers // 2
    return pl.pallas_call(
        turn_kernel,
        out_shape=[jax.ShapeDtypeStruct((width // peers, rows), BF16)] * slots,
        grid_spec=pltpu.PrefetchScalarGridSpec(
            num_scalar_prefetch=1,
            grid=(1,),
            in_specs=[pl.BlockSpec((rows, width // 2), lambda i, at: (0, (at[0] // slots) ^ far))],
            out_specs=[WHOLE] * slots,
            scratch_shapes=[pltpu.VMEM((width // 2, rows), BF16)],
        ),
        compiler_params=pltpu.CompilerParams(vmem_limit_bytes=12 << 20),
        cost_estimate=pl.CostEstimate(flops=0, bytes_accessed=2 * rows * width, transcendentals=0),
    )(at, feats)


def reverse_bits(value, size):
    out = jnp.zeros_like(value)
    bit = 1
    while bit < size:
        out = out * 2 + (value // bit) % 2
        bit *= 2
    return out


def edges_kernel(slots, first, spans, at, meta, *refs):
    x_refs = refs[: len(slots)]
    tiles_ref = refs[len(slots)]
    rest = refs[len(slots) + 1 :]
    tile = LANES
    edges = meta.shape[2]
    _, rows = x_refs[0].shape
    blocks = rows // tile
    if first and spans:
        out_refs, acc_ref = rest[:-1], rest[-1]
        acc_ref[...] = jnp.zeros_like(acc_ref)
    elif first:
        acc_ref = rest[0]
        acc_ref[...] = jnp.zeros_like(acc_ref)
    else:
        out_refs, acc_ref = rest[1:-1], rest[-1]
        acc_ref[...] = rest[0][...]
    for slot, x_ref in zip(slots, x_refs):
        for base in range(0, edges, 32):
            values = []
            for e in range(base, min(base + 32, edges)):
                source = x_ref[:, pl.ds(pl.multiple_of(meta[slot, 0, e], tile), tile)]
                value = jnp.dot(source, tiles_ref[meta[slot, 2, e]], preferred_element_type=F32)
                values.append(value.astype(BF16).astype(F32))
            for i, value in enumerate(values):
                acc_ref[meta[slot, 1, base + i]] += value
    peers = meta.shape[0]
    begin = 0
    for chunk, span in enumerate(spans):
        for k in range(peers):
            start = (at[0] ^ k) * blocks + begin
            for block in range(span):
                out_refs[chunk * peers + k][:, block * tile : (block + 1) * tile] = acc_ref[
                    start + block
                ].astype(BF16)
        begin += span


def sum_edges(at, meta, xs, slots, tiles, held, spans):
    part, rows = xs[0].shape
    peers, _, edges = meta.shape
    total = (peers * (rows // LANES), part, LANES)
    if spans:
        shapes = [jax.ShapeDtypeStruct((part, n * LANES), BF16) for n in spans for _ in range(peers)]
        scratch = [pltpu.VMEM(total, F32)]
    else:
        shapes, scratch = [jax.ShapeDtypeStruct(total, F32)], []
    operands = list(xs) + [tiles] + ([] if held is None else [held])
    return pl.pallas_call(
        functools.partial(edges_kernel, slots, held is None, spans),
        out_shape=shapes,
        grid_spec=pltpu.PrefetchScalarGridSpec(
            num_scalar_prefetch=2,
            grid=(),
            in_specs=[WHOLE] * len(operands),
            out_specs=[WHOLE] * len(shapes),
            scratch_shapes=scratch,
        ),
        compiler_params=pltpu.CompilerParams(vmem_limit_bytes=24 << 20),
        cost_estimate=pl.CostEstimate(
            flops=2 * len(slots) * edges * LANES * LANES * part,
            bytes_accessed=2 * len(slots) * (part * rows + 8 * LANES * LANES),
            transcendentals=0,
        ),
    )(at, meta, *operands)


def head_kernel(peers, base, first, last, at, *refs):
    a_refs = refs[:peers]
    feats_ref, cot_ref, weights_ref = refs[peers : peers + 3]
    refs = refs[peers + 3 :]
    if not first:
        held = refs[1:3]
        refs = refs[3:]
    count = 5 if last else 3
    out_ref, *sum_refs = refs[:count]
    agg_ref, x_ref, c_ref, w_ref, pre_ref, made_ref, grad_ref, *refs = refs[count:]
    totals, in_sem, out_sem = refs[:2], refs[2], refs[3]
    if last:
        gives = refs[4:6]
    width, span = agg_ref.shape
    part = width // peers
    step = 256 if span % 256 == 0 else 128
    stores = []

    def fetch(source, place, slot):
        copy = pltpu.make_async_copy(source, place, in_sem.at[slot])
        copy.start()
        return copy

    def store(source, place):
        copy = pltpu.make_async_copy(source, place, out_sem.at[len(stores)])
        copy.start()
        stores.append(copy)

    own_rows = pl.ds(base, span)
    early = [fetch(feats_ref.at[own_rows], x_ref, peers), fetch(weights_ref, w_ref, peers + 1)]
    parts = []
    for k in range(peers):
        place = agg_ref.at[pl.ds(pl.multiple_of((at[0] ^ k) * part, part), part)]
        parts.append(fetch(a_refs[k], place, k))
    parts.append(fetch(cot_ref.at[own_rows], c_ref, peers + 2))
    late = []
    if not first:
        late = [fetch(ref, total, peers + 3 + i) for i, (ref, total) in enumerate(zip(held, totals))]
    for copy in early:
        copy.wait()
    pre_ref[...] = jnp.dot(x_ref[...], w_ref[:, :width], preferred_element_type=F32)
    for copy in parts:
        copy.wait()

    over_rows = (((0,), (0,)), ((), ()))
    for i in range(span // step):
        here = slice(i * step, (i + 1) * step)
        pre = pre_ref[here] + lax.dot_general(
            agg_ref[:, here], w_ref[:, width:], over_rows, preferred_element_type=F32
        )
        scale = lax.rsqrt(jnp.mean(pre * pre, -1, keepdims=True) + 1e-05)
        normed = pre * scale
        gate = jax.nn.sigmoid(normed)
        made_ref[here] = (normed * gate).astype(BF16)
        store(made_ref.at[here], out_ref.at[base + i * step : base + (i + 1) * step])
        slope = c_ref[here].astype(F32)
        slope = slope * (gate * (1.0 + normed * (1.0 - gate)))
        grad = scale * (slope - normed * jnp.mean(slope * normed, -1, keepdims=True))
        grad_ref[here] = grad.astype(BF16)

    for copy in late:
        copy.wait()
    grad = grad_ref[...]
    for i, total in enumerate(totals):
        if i == 0:
            term = lax.dot_general(x_ref[...], grad, over_rows, preferred_element_type=F32)
        else:
            term = jnp.dot(agg_ref[...], grad, preferred_element_type=F32)
        total[...] = term if first else total[...] + term
        if not last:
            store(total, sum_refs[i])
            continue
        keep, give = sum_refs[i], sum_refs[2 + i]
        pairs, share, _ = keep.shape
        side = at[1] % 2
        for pair in range(pairs):
            here = pl.multiple_of((2 * pair + side) * share, share)
            there = pl.multiple_of((2 * pair + 1 - side) * share, share)
            gives[i][pair] = total[pl.ds(there, share)].astype(BF16)
            store(total.at[pl.ds(here, share)], keep.at[pair])
        store(gives[i], give)
    for copy in stores:
        copy.wait()


def run_head(at, parts, feats, cot, weights, hidden, held, base, span, configs):
    peers = len(parts)
    rows, width = feats.shape
    first, last = base == 0, base + span == rows
    step = 256 if span % 256 == 0 else 128
    shapes = [jax.ShapeDtypeStruct((rows, width), BF16)]
    sums = (width, width)
    scratch = [
        pltpu.VMEM((width, span), BF16),
        pltpu.VMEM((span, width), BF16),
        pltpu.VMEM((span, width), BF16),
        pltpu.VMEM((width, 2 * width), BF16),
        pltpu.VMEM((span, width), F32),
        pltpu.VMEM((span, width), BF16),
        pltpu.VMEM((span, width), BF16),
        pltpu.VMEM(sums, F32),
        pltpu.VMEM(sums, F32),
        pltpu.SemaphoreType.DMA((peers + 5,)),
        pltpu.SemaphoreType.DMA((span // step + (2 + configs if last else 2),)),
    ]
    if last:
        share = (configs // 2, width // configs, width)
        shapes += [jax.ShapeDtypeStruct(share, F32)] * 2 + [jax.ShapeDtypeStruct(share, BF16)] * 2
        scratch += [pltpu.VMEM(share, BF16)] * 2
    else:
        shapes += [jax.ShapeDtypeStruct(sums, F32)] * 2
    operands = [*parts, feats, cot, weights] + ([] if first else [hidden, *held])
    return pl.pallas_call(
        functools.partial(head_kernel, peers, base, first, last),
        out_shape=shapes,
        grid_spec=pltpu.PrefetchScalarGridSpec(
            num_scalar_prefetch=1,
            grid=(),
            in_specs=[STAYS] * len(operands),
            out_specs=[STAYS] * len(shapes),
            scratch_shapes=scratch,
        ),
        input_output_aliases={} if first else {peers + 4: 0},
        compiler_params=pltpu.CompilerParams(vmem_limit_bytes=60 << 20),
        cost_estimate=pl.CostEstimate(
            flops=8 * span * width * width, bytes_accessed=8 * span * width, transcendentals=span * width
        ),
    )(at, *operands)


def local(features, cotangent, w_self, w_neigh, tiles, edge_peer, edge_src, edge_dst, edge_tile):
    return layer(
        features[0], cotangent[0], w_self, w_neigh, tiles, edge_peer, edge_src, edge_dst, edge_tile
    )


def layer(feats, cot, w_self, w_neigh, tiles, edge_peer, edge_src, edge_dst, edge_tile):
    rows, width = feats.shape
    count, tile, _ = tiles.shape
    edges = edge_src.shape[0]
    assert tile == LANES and edges <= LANES
    peers = lax.axis_size("dom")
    configs = lax.axis_size("cfg")
    assert configs % 2 == 0 and peers % 2 == 0
    own = lax.axis_index("cfg")
    at = jnp.stack([lax.axis_index("dom"), own]).astype(I32)
    blocks = rows // tile
    spans = [blocks - blocks // 2, blocks // 2] if blocks > 2 else [blocks]
    chunks = len(spans)
    dom_bits, cfg_bits = bits_of("dom"), bits_of("cfg")
    middle = peers // 2

    piece = count * tile // configs
    per = piece // tile if piece % tile == 0 else count
    pack = pl.pallas_call(
        pack_kernel,
        out_shape=jax.ShapeDtypeStruct((piece + 16, tile), BF16),
        grid_spec=pltpu.PrefetchScalarGridSpec(
            num_scalar_prefetch=0,
            grid=(),
            in_specs=[STAYS] * 5,
            out_specs=WHOLE,
            scratch_shapes=[
                pltpu.VMEM((per, tile, tile), BF16),
                pltpu.VMEM((count * tile, tile), BF16),
                pltpu.VMEM((4, 1, edges), I32),
                pltpu.VMEM((16, tile), F32),
                pltpu.SemaphoreType.DMA((5,)),
            ],
        ),
        compiler_params=pltpu.CompilerParams(vmem_limit_bytes=60 << 20),
        name="pack",
    )
    lists = [each.reshape(1, edges) for each in (edge_peer, edge_src, edge_dst, edge_tile)]
    packed = pack(tiles, *lists)
    far_turned = turn_half(at, feats, peers, 1)
    near_turned = turn_half(at, feats, peers, 0)

    evens = [k for k in range(peers) if k % 2 == 0]
    held = jnp.stack([packed] + [swap(packed, "dom", k) for k in evens[1:]])
    held = jnp.concatenate([held, swap(held, "dom", 1)], 0)
    offsets = evens + [k + 1 for k in evens]
    slot = {k: offsets.index(k) for k in range(peers)}
    quarters = held[:, :piece]
    pieces = jnp.concatenate([quarters[None], swap(quarters[None], "cfg", cfg_bits[-1])], 0)
    for bit in cfg_bits[:-1][::-1]:
        pieces = jnp.concatenate([pieces, swap(pieces, "cfg", bit)], 0)

    infos = held[:, piece : piece + 4, :edges].astype(I32)
    slot_of = jnp.arange(peers, dtype=I32)[:, None]
    if piece % tile == 0:
        owner = reverse_bits((infos[:, 3] // per) ^ own, configs)
        which = (owner * peers + slot_of) * per + infos[:, 3] % per
        all_tiles = pieces.reshape(peers * count, tile, tile)
    else:
        which = slot_of * count + infos[:, 3]
        order = reverse_bits(jnp.arange(configs, dtype=I32) ^ own, configs)
        all_tiles = pieces[order].swapaxes(0, 1).reshape(peers * count, tile, tile)
    meta = jnp.stack([infos[:, 1] * tile, infos[:, 0] * blocks + infos[:, 2], which], 1)

    moved = {0: near_turned[0]}
    for k in range(1, peers):
        block = far_turned[k - middle] if k >= middle else near_turned[k]
        moved[k] = swap(block, "dom", k)

    weights = jnp.concatenate([w_self, w_neigh], 1)[None]
    for bit in cfg_bits[::-1]:
        weights = jnp.concatenate([weights, swap(weights, "cfg", bit)], 0)
    order = reverse_bits(jnp.arange(configs, dtype=I32) ^ own, configs)
    weights = weights[order].reshape(width, 2 * width)

    near, far = list(range(middle)), list(range(middle, peers))
    partly = sum_edges(at, meta, [moved[k] for k in near], [slot[k] for k in near], all_tiles, None, [])[0]
    summed = sum_edges(at, meta, [moved[k] for k in far], [slot[k] for k in far], all_tiles, partly, spans)
    held = hidden = None
    for chunk in range(chunks):
        parts = summed[chunk * peers : (chunk + 1) * peers]
        back = [parts[0]] + [swap(parts[k], "dom", k) for k in range(1, peers)]
        hidden, *held = run_head(
            at, back, feats, cot, weights, hidden, held, sum(spans[:chunk]) * tile, spans[chunk] * tile, configs
        )
    keep_s, keep_n, give_s, give_n = held
    factor = float(configs * peers * rows) ** (-0.5)

    def reduce(keep, give, order):
        here = [keep, swap(give, "cfg", cfg_bits[0])]
        for bit in cfg_bits[1:]:
            side = (own // bit) % 2

            def pick(which):
                halves = [each.reshape((each.shape[0] // 2, 2) + each.shape[1:]) for each in here]
                halves = [lax.dynamic_index_in_dim(each, which, 1, keepdims=False) for each in halves]
                return halves[0] + halves[1].astype(F32)

            here = [pick(side), swap(pick(1 - side).astype(BF16), "cfg", bit)]
        total = (here[0] + here[1].astype(F32))[0]
        for bit in order:
            total = total + swap(total.astype(BF16), "dom", bit).astype(F32)
        return total * factor

    grad_s = reduce(keep_s, give_s, dom_bits)
    grad_n = reduce(keep_n, give_n, dom_bits[1:] + dom_bits[:1])
    return (hidden[None], grad_s, grad_n)


def solution(mesh):
    placed = (
        P("cfg", "dom", None),
        P("cfg", "dom", None),
        P("cfg", None),
        P("cfg", None),
        P("dom", None, None),
        P("dom", None),
        P("dom"),
        P("dom"),
        P("dom"),
    )
    return jax.shard_map(
        local,
        mesh=mesh,
        in_specs=placed,
        out_specs=(P("cfg", "dom", None), P("cfg", None), P("cfg", None)),
        check_vma=False,
    )
```
